32 devices in a mesh: pipe: 4 (over y, x), expert: 8 (over z, core).
Axes of the slice: x: 2, y: 2, z: 4, core: 2. Of those that a mesh axis runs over, the one named last changes fastest.
Arguments:
- activations: bfloat16 [4, 1024, 2560], P('pipe', 'expert'), may hold values from -6 to 6
- out_grad: bfloat16 [4, 1024, 2560], P('pipe', 'expert'), may hold values from -6 to 6
- expert_ids: int32 [4, 1024, 2], P('pipe', 'expert'), may hold values from 0 to 3, all different within a row; in each aligned block of 128 rows (0 to 127, 128 to 255, ..., all dimensions but the last counted through in order) at most 96 rows name the same one
- gate_values: float32 [4, 1024, 2], P('pipe', 'expert'), may hold values from 0.1 to 1
- w_gate: bfloat16 [4, 2560, 3072], P('pipe', None, 'expert'), may hold values from -0.125 to 0.125
- w_up: bfloat16 [4, 2560, 3072], P('pipe', None, 'expert'), may hold values from -0.125 to 0.125
- w_down: bfloat16 [4, 3072, 2560], P('pipe', 'expert'), may hold values from -0.21875 to 0.21875
Outputs:
- passed_grad: bfloat16 [4, 1024, 2560], P('pipe', 'expert')
- router_grad: float32 [4, 1024, 2], P('pipe', 'expert')
The draws below stay inside these ranges and needn't reach their ends.
Inputs may be any that keep to these rules, and one draw needn't show every extreme that they name: `expert_ids`: each row names 2 different experts. In the 128 rows of one section on one device (aligned blocks of rows) no expert is named by more than 96 rows, a bound that some block reaches; every expert is named somewhere.
All inputs are finite; a program needn't handle non-finite values.
Results may differ from the reference program's by a relative error of at most 0.0095.
Values may be sent and summed in bfloat16 or wider, within the bound.
A program may use at most 128 MiB of HBM per device.

```python
import math
import jax
import jax.numpy as jnp
import numpy as np
from jax import lax

D = 2560
HID = 768
TOP = 2
TOK_DEV = 128
EXPERTS = 4
SECTIONS = 4
TOKENS = 1024
CAP = 96
N_EXPERT = 8


def level_of(stream_key, extent, pieces, smallest, high):
    gain, own = 1.0, jax.random.fold_in(stream_key, 6)
    for axis_at, blocks in pieces:
        heights = jnp.exp(jax.random.uniform(jax.random.fold_in(own, axis_at), (blocks,), jnp.float32, smallest / len(pieces), high / len(pieces)))
        gain = gain * jnp.repeat(heights, extent[axis_at] // blocks).reshape([-1 if axis == axis_at else 1 for axis in range(len(extent))])
    return gain


def assign_block(rng, own, number, rows, number_of, top, bound, skew):
    sequence = jax.random.permutation(rng, number_of)
    crowded, usual = portions_of(number_of, rows * top, bound, skew, True), portions_of(number_of, rows * top, bound, skew, False)
    places = jnp.arange(number_of)

    def named(sizes, rotation):
        used = int((sizes > 0).sum())
        fixed = max(1, used // 4)
        shifted = fixed + (places - fixed + rotation * (used - fixed)) % max(1, number_of - fixed)
        return jnp.zeros((number_of,), jnp.int32).at[sequence[jnp.where(places < fixed, places, shifted)]].set(jnp.asarray(sizes, jnp.int32))

    sizes = jnp.where(number % 4 == 0, named(crowded, number // 4), named(usual, number - number // 4 - 1))
    mixed = jax.random.permutation(jax.random.fold_in(own, 3), number_of)
    source_of, sink = mixed[0:number_of // 2 * 2:2], mixed[1:number_of // 2 * 2:2]
    slack = jnp.minimum(sizes[source_of] - 1, bound - sizes[sink]) // 2
    slack = jnp.where((source_of == sequence[0]) | (sink == sequence[0]) | (sizes[sink] == 0), 0, jnp.maximum(slack, 0))
    shifted = jax.random.randint(jax.random.fold_in(own, 4), (number_of // 2,), 0, 1 << 20) % (slack + 1)
    sizes = sizes.at[source_of].add(-shifted).at[sink].add(shifted)
    labels = jnp.searchsorted(jnp.cumsum(sizes), jnp.arange(rows * top), side="right").astype(jnp.int32)
    grid = labels.reshape(top, rows).T
    grid = grid[jax.random.permutation(jax.random.fold_in(own, 1), rows)]
    rotation = jax.random.randint(jax.random.fold_in(own, 2), (rows, 1), 0, top)
    return jnp.take_along_axis(grid, (jnp.arange(top)[None, :] + rotation) % top, axis=1)


def portions_of(count, total, most, skew, full):
    loads = [(1 << 20) // math.isqrt(standing ** skew) + 1 for standing in range(1, count + 1)]
    largest = most if full else min(most, max(-(-total // count), total * loads[0] // sum(loads)))
    least = 1 if total - largest >= count - 1 else 0
    holding, rest = [largest] + [least] * (count - 1), total - largest - least * (count - 1)
    while rest > 0:
        movable = [i for i in range(1, count) if holding[i] < largest] or [i for i in range(1, count) if holding[i] < most]
        pool, left = sum([loads[i] for i in movable]), rest
        for i in movable:
            addition = min(most - holding[i], max(1, left * loads[i] // pool), rest)
            holding[i] = holding[i] + addition
            rest = rest - addition
    return np.array(holding)


def normal_values(stream_key, extent, deviation, bound, pieces=(), held_as=jnp.bfloat16):
    array = deviation * jax.random.normal(stream_key, extent, jnp.float32)
    if pieces:
        array = array * level_of(stream_key, extent, pieces, -0.22, 0.18)
    return jnp.clip(array, -bound, bound).astype(held_as)


def setup_inputs(seed: int = 0) -> dict:
    arg_keys = jax.random.split(jax.random.key(seed), 8)
    activations = normal_values(arg_keys[0], (SECTIONS, TOKENS, D), 1.0, 6.0, ((0, 4), (1, 8)))
    out_grad = normal_values(arg_keys[1], (SECTIONS, TOKENS, D), 1.0, 6.0, ((0, 4), (1, 8)))
    expert_ids_keys = jax.random.split(jax.random.fold_in(arg_keys[2], 1), SECTIONS * TOKENS // TOK_DEV)
    expert_ids_turns = jax.random.permutation(jax.random.fold_in(arg_keys[2], 3), SECTIONS * TOKENS // TOK_DEV)
    expert_ids = jax.vmap(lambda own, number: assign_block(jax.random.fold_in(arg_keys[2], 2), own, number, TOK_DEV, EXPERTS, TOP, CAP, 2))(expert_ids_keys, expert_ids_turns).reshape((SECTIONS, TOKENS, TOP))
    gate_values = jnp.clip(0.1 + 0.9 * jax.random.uniform(arg_keys[3], (SECTIONS, TOKENS, TOP), jnp.float32) ** level_of(arg_keys[3], (SECTIONS, TOKENS, TOP), ((0, 4), (1, 8)), -0.2, 0.2), 0.1, 1.0)
    w_gate = normal_values(arg_keys[4], (SECTIONS, D, EXPERTS * HID), D ** -0.5, 0.125, ((0, 4), (2, 8)))
    w_up = normal_values(arg_keys[5], (SECTIONS, D, EXPERTS * HID), D ** -0.5, 0.125, ((0, 4), (2, 8)))
    w_down = normal_values(arg_keys[6], (SECTIONS, EXPERTS * HID, D), HID ** -0.5, 0.21875, ((0, 4), (1, 8)))
    return dict(activations=activations, out_grad=out_grad, expert_ids=expert_ids, gate_values=gate_values, w_gate=w_gate, w_up=w_up, w_down=w_down)


def route_terms(rows_in, rows_grad, gate_cols, up_cols, down_rows):
    contract = (((1,), (1,)), ((), ()))
    gate_pre = jnp.dot(rows_in, gate_cols, preferred_element_type=jnp.float32)
    up_pre = jnp.dot(rows_in, up_cols, preferred_element_type=jnp.float32)
    squash = jax.nn.sigmoid(gate_pre)
    activated = gate_pre * squash
    hidden = (activated * up_pre).astype(jnp.bfloat16)
    back_hidden = lax.dot_general(rows_grad, down_rows, contract, preferred_element_type=jnp.float32)
    router_part = jnp.sum(hidden.astype(jnp.float32) * back_hidden, axis=1)
    slope = squash * (1.0 + gate_pre * (1.0 - squash))
    grad_gate = (back_hidden * up_pre * slope).astype(jnp.bfloat16)
    grad_up = (back_hidden * activated).astype(jnp.bfloat16)
    route_part = lax.dot_general(grad_gate, gate_cols, contract, preferred_element_type=jnp.float32)
    route_part = route_part + lax.dot_general(grad_up, up_cols, contract, preferred_element_type=jnp.float32)
    return route_part, router_part


def section_grads(inputs, grads_out, routes, weights_gate, gate_all, up_all, down_all):
    entries = TOKENS * TOP
    capacity = N_EXPERT * CAP
    flat_ids = routes.reshape(-1).astype(jnp.int32)
    one_hot = (flat_ids[:, None] == jnp.arange(EXPERTS, dtype=jnp.int32)[None, :]).astype(jnp.int32)
    slot_rank = jnp.sum((jnp.cumsum(one_hot, axis=0) - 1) * one_hot, axis=1).astype(jnp.int32)
    slot_index = (flat_ids * capacity + slot_rank).astype(jnp.int32)
    slot_table = jnp.full((EXPERTS * capacity,), entries, jnp.int32).at[slot_index].set(jnp.arange(entries, dtype=jnp.int32))
    slot_table = slot_table.reshape(EXPERTS, capacity)
    padded_in = jnp.concatenate([inputs, jnp.zeros((1, D), inputs.dtype)], 0)
    padded_grad = jnp.concatenate([grads_out, jnp.zeros((1, D), grads_out.dtype)], 0)

    def one_expert(expert_index):
        token_of = (slot_table[expert_index] // TOP).astype(jnp.int32)
        start = (expert_index * HID).astype(jnp.int32)
        gate_cols = lax.dynamic_slice_in_dim(gate_all, start, HID, 1)
        up_cols = lax.dynamic_slice_in_dim(up_all, start, HID, 1)
        down_rows = lax.dynamic_slice_in_dim(down_all, start, HID, 0)
        return route_terms(padded_in[token_of], padded_grad[token_of], gate_cols, up_cols, down_rows)

    route_all, router_all = lax.map(one_expert, jnp.arange(EXPERTS, dtype=jnp.int32))
    entry_route = route_all.reshape(EXPERTS * capacity, D)[slot_index]
    entry_router = router_all.reshape(-1)[slot_index]
    input_grad = jnp.sum(weights_gate.reshape(TOKENS, TOP, 1) * entry_route.reshape(TOKENS, TOP, D), axis=1)
    return input_grad.astype(jnp.bfloat16), entry_router.reshape(TOKENS, TOP)


def reference(activations, out_grad, expert_ids, gate_values, w_gate, w_up, w_down):
    input_list = []
    router_list = []
    for section_index in range(SECTIONS):
        input_grad, router_part = section_grads(activations[section_index], out_grad[section_index], expert_ids[section_index], gate_values[section_index], w_gate[section_index], w_up[section_index], w_down[section_index])
        input_list.append(input_grad)
        router_list.append(router_part)
    input_list.append(jnp.zeros((TOKENS, D), jnp.bfloat16))
    passed_grad = jnp.stack(input_list[1:], 0)
    router_grad = jnp.stack(router_list, 0)
    return passed_grad, router_grad
```

```python
import functools

import jax
import jax.numpy as jnp
from jax import lax
from jax.experimental import pallas as pl
from jax.experimental.pallas import tpu as pltpu
from jax.sharding import PartitionSpec as P


def shifted(block, axis, distance):
    devices = range(lax.axis_size(axis))
    route = [(i - distance, i) for i in devices if i - distance in devices]
    return lax.ppermute(block, axis, route)


def expert_terms(rows_in, rows_grad, gate_cols, up_cols, down_rows):
    contract = (((1,), (1,)), ((), ()))
    gate_pre = jnp.dot(rows_in, gate_cols, preferred_element_type=jnp.float32)
    up_pre = jnp.dot(rows_in, up_cols, preferred_element_type=jnp.float32)
    squash = jax.nn.sigmoid(gate_pre)
    activated = gate_pre * squash
    hidden = (activated * up_pre).astype(jnp.bfloat16)
    back_hidden = lax.dot_general(
        rows_grad, down_rows, contract, preferred_element_type=jnp.float32
    )
    router_part = jnp.sum(hidden.astype(jnp.float32) * back_hidden, axis=1)
    slope = squash * (1.0 + gate_pre * (1.0 - squash))
    grad_gate = (back_hidden * up_pre * slope).astype(jnp.bfloat16)
    grad_up = (back_hidden * activated).astype(jnp.bfloat16)
    route_part = lax.dot_general(grad_gate, gate_cols, contract, preferred_element_type=jnp.float32)
    route_part = route_part + lax.dot_general(
        grad_up, up_cols, contract, preferred_element_type=jnp.float32
    )
    return (route_part, router_part)


def routed_local(activations, out_grad, expert_ids, gate_values, w_gate, w_up, w_down):
    inputs = activations[0]
    grads_out = out_grad[0]
    routes = expert_ids[0]
    weights_gate = gate_values[0]
    gate_local = w_gate[0]
    up_local = w_up[0]
    down_local = w_down[0]
    devices_e = lax.axis_size("expert")
    owners = devices_e // 2
    tokens_dev, top_k = routes.shape
    feat_width = inputs.shape[1]
    capacity = min(tokens_dev * 3 // 4, tokens_dev * top_k * 3 // (2 * owners))
    count_entries = tokens_dev * top_k
    flat_ids = routes.reshape(-1)
    one_hot = (flat_ids[:, None] == jnp.arange(owners, dtype=jnp.int32)[None, :]).astype(jnp.int32)
    slot_rank = jnp.sum((jnp.cumsum(one_hot, axis=0) - 1) * one_hot, axis=1)
    slot_index = flat_ids * capacity + slot_rank
    slot_table = (
        jnp.full((owners * capacity,), count_entries, jnp.int32)
        .at[slot_index]
        .set(jnp.arange(count_entries, dtype=jnp.int32))
    )
    token_of = slot_table // top_k
    pad_row = jnp.zeros((1, feat_width), inputs.dtype)
    send_in = jnp.concatenate([inputs, pad_row], 0)[token_of].reshape(owners, capacity, feat_width)
    send_grad = jnp.concatenate([grads_out, pad_row], 0)[token_of].reshape(
        owners, capacity, feat_width
    )
    full_in = lax.all_to_all(
        jnp.repeat(send_in, 2, axis=0), "expert", split_axis=0, concat_axis=0, tiled=True
    )
    item_count = full_in.shape[1]
    route_part, router_part = expert_terms(
        full_in.reshape(-1, feat_width),
        lax.all_to_all(
            jnp.repeat(send_grad, 2, axis=0), "expert", split_axis=0, concat_axis=0, tiled=True
        ).reshape(-1, feat_width),
        gate_local,
        up_local,
        down_local,
    )
    route_part = route_part.reshape(devices_e, item_count, feat_width)
    router_part = router_part.reshape(devices_e, item_count)
    back_route = lax.all_to_all(
        route_part.astype(jnp.bfloat16), "expert", split_axis=0, concat_axis=0, tiled=True
    ).astype(route_part.dtype)
    back_router = lax.all_to_all(
        router_part.astype(jnp.bfloat16), "expert", split_axis=0, concat_axis=0, tiled=True
    ).astype(router_part.dtype)
    summed = jnp.sum(back_route.reshape(owners, 2, item_count, feat_width), axis=1)
    router_sum = jnp.sum(back_router.reshape(owners, 2, item_count), axis=1)
    route_sum, router_sum = (summed, router_sum)
    entry_route = route_sum.reshape(-1, feat_width)[slot_index]
    entry_router = router_sum.reshape(-1)[slot_index]
    input_grad = jnp.sum(
        weights_gate.reshape(tokens_dev, top_k, 1)
        * entry_route.reshape(tokens_dev, top_k, feat_width),
        axis=1,
    ).astype(jnp.bfloat16)
    passed = shifted(input_grad, "pipe", -1)
    return (passed[None], entry_router.reshape(tokens_dev, top_k)[None])


MESH = pl.DeviceIdType.MESH
NT = (((1,), (1,)), ((), ()))


def line_kernel(
    n, cap, sx_ref, sg_ref, wt_ref, pt_ref, wg_hbm, wu_hbm, wd_hbm, out_ref, rr_ref,
    xa, ga, xb, gb, xo, go, wgu, wd, wp, pre, gs, gr, part, ca, cb, ta, tb, fin, wts, pts, rl, rs,
    w_sem, o_ssem, rn_sem, a_ssem, a_psem, ra_sem, b_ssem, b_psem, rb_sem, wt_ssem, wt_rsem,
    pt_ssem, pt_rsem, wp_ssem, wp_rsem, g_ssem, g_rsem, ca_ssem, ca_rsem, cb_ssem, cb_rsem,
    rr_ssem, rr_rsem, f_ssem, f_rsem,
):
    stage = lax.axis_index("pipe")
    me = lax.axis_index("expert")
    stages = lax.axis_size("pipe")
    c, k = lax.div(me, 2), lax.rem(me, 2)
    other = 1 - k
    tok = sx_ref.shape[1]
    rest = tok - cap
    hid = wd.shape[0]
    half_d = wp.shape[0]
    partner = (stage, c * 2 + other)
    send, land_a, land_b, land_o = (sx_ref, sg_ref), (xa, ga), (xb, gb), (xo, go)

    def rdma(src, dst, ssem, rsem, dev):
        return pltpu.make_async_remote_copy(
            src_ref=src, dst_ref=dst, send_sem=ssem, recv_sem=rsem, device_id=dev, device_id_type=MESH
        )

    loads = [
        pltpu.make_async_copy(wg_hbm, wgu.at[:, pl.ds(0, hid)], w_sem.at[0]),
        pltpu.make_async_copy(wu_hbm, wgu.at[:, pl.ds(hid, hid)], w_sem.at[1]),
        pltpu.make_async_copy(wd_hbm, wd, w_sem.at[2]),
    ]
    for load in loads:
        load.start()
    rl[...] = jnp.zeros_like(rl)

    barrier = pltpu.get_barrier_semaphore()
    for j in range(1, 2 * n):
        pl.semaphore_signal(barrier, inc=1, device_id=(stage, lax.rem(me + j, 2 * n)), device_id_type=MESH)
    for kk in range(2):

        @pl.when(stage > 0)
        def _():
            pl.semaphore_signal(barrier, inc=1, device_id=(stage - 1, c * 2 + kk), device_id_type=MESH)

        @pl.when(stage < stages - 1)
        def _():
            pl.semaphore_signal(barrier, inc=1, device_id=(stage + 1, c * 2 + kk), device_id_type=MESH)

    near = (stage > 0).astype(jnp.int32) + (stage < stages - 1).astype(jnp.int32)
    pl.semaphore_wait(barrier, 2 * n - 1 + 2 * near)

    def mirrored(s, chip):
        return chip if s == 0 else n - 1 - chip

    def onward(s):
        return (stage, (c + 1 - 2 * s) * 2 + k)

    def backward(s):
        return (stage, (c - 1 + 2 * s) * 2 + k)

    def own_a(s, h):
        return rdma(send[h].at[s, pl.ds(0, cap)], land_a[h].at[c, pl.ds(k * cap, cap)],
                    a_ssem.at[s, c, h], ra_sem.at[me, h], onward(s))

    def fwd_a(s, t, h):
        view = land_a[h].at[t, pl.ds(k * cap, cap)]
        return rdma(view, view, a_ssem.at[s, t, h], ra_sem.at[t * 2 + k, h], onward(s))

    def pair_a(t, h):
        view = land_a[h].at[t, pl.ds(k * cap, cap)]
        return rdma(view, view, a_psem.at[t, h], ra_sem.at[t * 2 + k, h], partner)

    def got_a(t, kk, h):
        view = land_a[h].at[t, pl.ds(kk * cap, cap)]
        return rdma(view, view, a_psem.at[t, h], ra_sem.at[t * 2 + kk, h], partner)

    def own_b(s, h):
        return rdma(send[h].at[s, pl.ds(cap, rest)], land_b[h].at[c, pl.ds(k * rest, rest)],
                    b_ssem.at[s, c, h], rb_sem.at[me, h], onward(s))

    def fwd_b(s, t, h):
        view = land_b[h].at[t, pl.ds(k * rest, rest)]
        return rdma(view, view, b_ssem.at[s, t, h], rb_sem.at[t * 2 + k, h], onward(s))

    def pair_b(t, h):
        view = land_b[h].at[t, pl.ds(k * rest, rest)]
        return rdma(view, view, b_psem.at[t, h], rb_sem.at[t * 2 + k, h], partner)

    def got_b(t, kk, h):
        view = land_b[h].at[t, pl.ds(kk * rest, rest)]
        return rdma(view, view, b_psem.at[t, h], rb_sem.at[t * 2 + kk, h], partner)

    def nat_copy(h):
        return rdma(send[h].at[2], land_o[h].at[pl.ds(k * tok, tok)], o_ssem.at[h], rn_sem.at[h], partner)

    def nat_here(h):
        return pltpu.make_async_copy(send[h].at[2], land_o[h].at[pl.ds(k * tok, tok)], o_ssem.at[2 + h])

    def wt_copy(j):
        return rdma(wt_ref, wts.at[me], wt_ssem.at[j], wt_rsem.at[me], (stage, lax.rem(me + j, 2 * n)))

    def wt_got(j):
        src = lax.rem(me + j, 2 * n)
        return rdma(wt_ref, wts.at[src], wt_ssem.at[j], wt_rsem.at[src], (stage, src))

    pt_copy = rdma(pt_ref, pts, pt_ssem, pt_rsem, partner)
    wp_copy = rdma(wgu.at[pl.ds(other * half_d, half_d)], wp, wp_ssem, wp_rsem, partner)

    for s in range(2):

        @pl.when(mirrored(s, c) < n - 1)
        def _():
            for h in range(2):
                own_a(s, h).start()

    for h in range(2):
        nat_copy(h).start()
        nat_here(h).start()
    for j in range(1, 2 * n):
        wt_copy(j).start()
    wts[me] = wt_ref[...]
    pt_copy.start()
    for load in loads:
        load.wait()
    wp_copy.start()

    def swap(slot, rows):
        return rdma(gs.at[slot, pl.ds(0, rows)], gr.at[slot, pl.ds(0, rows)], g_ssem.at[slot], g_rsem.at[slot], partner)

    def column(v):
        return jnp.transpose(jnp.broadcast_to(v, (v.shape[1], v.shape[1])))[:, :1]

    def terms(x_view, g_view, rows, slot, put_router):
        step = 256 if (2 * hid) % 256 == 0 else 128

        @pl.loop(0, 2 * hid // step)
        def _(j):
            cols = pl.ds(pl.multiple_of(j * step, step), step)
            pre[pl.ds(0, rows), cols] = jnp.dot(x_view[...], wgu[:, cols], preferred_element_type=jnp.float32)

        pre[pl.ds(0, rows), pl.ds(2 * hid, hid)] = lax.dot_general(
            g_view[...], wd[...], NT, preferred_element_type=jnp.float32
        )
        chunk = 32

        @pl.loop(0, rows // chunk)
        def _(i):
            at = pl.ds(pl.multiple_of(i * chunk, chunk), chunk)
            gate_pre = pre[at, pl.ds(0, hid)]
            up_pre = pre[at, pl.ds(hid, hid)]
            back = pre[at, pl.ds(2 * hid, hid)]
            squash = jax.nn.sigmoid(gate_pre)
            activated = gate_pre * squash
            hidden = (activated * up_pre).astype(jnp.bfloat16)
            router = jnp.sum(hidden.astype(jnp.float32) * back, axis=1, keepdims=True)
            slope = squash * (1.0 + gate_pre * (1.0 - squash))
            gs[slot, at, pl.ds(0, hid)] = (back * up_pre * slope).astype(jnp.bfloat16)
            gs[slot, at, pl.ds(hid, hid)] = (back * activated).astype(jnp.bfloat16)
            pre[at, pl.ds(0, 128)] = jnp.broadcast_to(router, (chunk, 128))

        swap(slot, rows).start()
        put_router()

    def products(rows, slot, weight):
        step = 256 if half_d % 256 == 0 else 128

        @pl.loop(0, half_d // step)
        def _(j):
            cols = pl.ds(pl.multiple_of(j * step, step), step)
            mine = pl.ds(pl.multiple_of(k * half_d + j * step, step), step)
            part[slot, pl.ds(0, rows), cols] = lax.dot_general(
                gs[slot, pl.ds(0, rows)], wgu[mine, :], NT, preferred_element_type=jnp.float32
            )

        swap(slot, rows).wait()

        @pl.loop(0, half_d // step)
        def _(j):
            cols = pl.ds(pl.multiple_of(j * step, step), step)
            total = part[slot, pl.ds(0, rows), cols] + lax.dot_general(
                gr[slot, pl.ds(0, rows)], wp[cols, :], NT, preferred_element_type=jnp.float32
            )
            part[slot, pl.ds(0, rows), cols] = total * weight

    def row_weights(t, base, lo, size):
        cols = [column(wts[t * 2 + kk, pl.ds(base + c, 1), :])[lo:lo + size] for kk in range(2)]
        return jnp.concatenate(cols, axis=0)

    for h in range(2):
        rdma(send[h].at[2], land_o[h].at[pl.ds(other * tok, tok)], o_ssem.at[h], rn_sem.at[h], partner).wait_recv()
        nat_here(h).wait()
    for j in range(1, 2 * n):
        wt_got(j).wait_recv()

    def own_router():
        for kk in range(2):
            rl[c * 2 + kk] = pre[pl.ds(kk * tok, tok), pl.ds(0, 128)]

    terms(xo, go, 2 * tok, n, own_router)
    wp_copy.wait_recv()
    products(2 * tok, n, row_weights(c, 2 * n, 0, tok))

    def chain_a(s, t):
        return rdma(ta.at[t], ca.at[s, t], ca_ssem.at[t], ca_rsem.at[s, t], backward(s))

    def chain_b(s, t):
        return rdma(tb.at[t], cb.at[s, t], cb_ssem.at[t], cb_rsem.at[s, t], backward(s))

    def real(s, chip):
        return chip if s == 0 else n - 1 - chip

    def chain_step(at):
        for s in range(2):
            here = mirrored(s, c)
            target = 2 * (n - 1) - here - at
            t = real(s, target)

            @pl.when((target >= 0) & (target < here))
            def _():
                @pl.when(here < n - 1)
                def _():
                    chain_a(s, t).wait_recv()
                    ta[t] = (part[t, pl.ds(0, 2 * cap)] + ca[s, t].astype(jnp.float32)).astype(jnp.bfloat16)

                @pl.when(here == n - 1)
                def _():
                    ta[t] = part[t, pl.ds(0, 2 * cap)].astype(jnp.bfloat16)

                chain_a(s, t).start()

    @pl.loop(1, n)
    def _(d):
        for s in range(2):
            here = mirrored(s, c)
            t = real(s, here - d)

            @pl.when(here >= d)
            def _():
                for h in range(2):
                    got_a(t, k, h).wait_recv()

                    @pl.when(here < n - 1)
                    def _():
                        fwd_a(s, t, h).start()

                    pair_a(t, h).start()

        for s in range(2):
            here = mirrored(s, c)

            @pl.when((here < n - 2) & (d == jnp.maximum(here, 1)))
            def _():
                for h in range(2):
                    own_b(s, h).start()

        @pl.loop(0, 2)
        def _(side):
            t = jnp.where(side == 0, c - d, c + d)

            @pl.when((t >= 0) & (t < n))
            def _():
                for h in range(2):
                    got_a(t, other, h).wait_recv()

                def put_router():
                    for kk in range(2):
                        rl[t * 2 + kk, pl.ds(0, cap)] = pre[pl.ds(kk * cap, cap), pl.ds(0, 128)]

                terms(xa.at[t], ga.at[t], 2 * cap, t, put_router)
                products(2 * cap, t, row_weights(t, side * n, 0, cap))

        for s in range(2):
            here = mirrored(s, c)
            back = jnp.where(here < n - 2, d, d - 1)
            t = real(s, here - back)

            @pl.when((here >= back) & (back > 0) & (here < n - 1))
            def _():
                for h in range(2):
                    got_b(t, k, h).wait_recv()

                    @pl.when(here < n - 2)
                    def _():
                        fwd_b(s, t, h).start()

                    pair_b(t, h).start()

        chain_step(d)

    inner = (c > 0) & (c < n - 1)

    @pl.when(inner)
    def _():
        for j in range(1, n):
            t = lax.rem(c + j, n)
            for h in range(2):
                got_b(t, other, h).wait_recv()

        def put_router():
            @pl.loop(0, n)
            def _(t):
                @pl.when(t != c)
                def _():
                    for kk in range(2):
                        rl[t * 2 + kk, pl.ds(cap, rest)] = pre[
                            pl.ds(pl.multiple_of(t * 2 * rest + kk * rest, rest), rest), pl.ds(0, 128)]

        rows_b = n * 2 * rest
        terms(xb.reshape(rows_b, xb.shape[2]), gb.reshape(rows_b, gb.shape[2]), rows_b, n + 1, put_router)
        weights = [row_weights(t, jnp.where(t < c, 0, n), cap, rest) for t in range(n)]
        products(rows_b, n + 1, jnp.concatenate(weights, axis=0))

    def chain_step_b(here_at):
        for s in range(2):
            here = mirrored(s, c)

            @pl.when(here == here_at)
            def _():
                for target in range(here_at):
                    t = real(s, target)
                    mine = part[n + 1, pl.ds(t * 2 * rest, 2 * rest)]
                    if here_at < n - 2:
                        chain_b(s, t).wait_recv()
                        mine = mine + cb[s, t].astype(jnp.float32)
                    tb[t] = mine.astype(jnp.bfloat16)
                    chain_b(s, t).start()

    for at in range(n, 2 * (n - 1)):
        chain_step(at)
        here_at = 2 * (n - 1) - at
        if 0 < here_at <= n - 2:
            chain_step_b(here_at)

    def rr_copy(j):
        dst = lax.rem(me + j, 2 * n)
        return rdma(rs.at[dst], rr_ref.at[me], rr_ssem.at[j], rr_rsem.at[me], (stage, dst))

    def rr_got(j):
        src = lax.rem(me + j, 2 * n)
        return rdma(rs.at[src], rr_ref.at[src], rr_ssem.at[j], rr_rsem.at[src], (stage, src))

    @pl.loop(0, 2 * n)
    def _(src):
        rs[src] = jnp.transpose(rl[src])[:8]

    for j in range(1, 2 * n):
        rr_copy(j).start()
    rr_ref[me] = rs[me]

    pt_copy.wait_recv()

    def place(s, rows_b):
        for kk in range(2):
            top = ca[s, c, pl.ds(kk * cap, cap)]
            low = cb[s, c, pl.ds(kk * rest, rest)] if rows_b else jnp.zeros((rest, half_d), jnp.bfloat16)
            spread = jnp.where(kk == k, pt_ref[s], pts[s])
            at = pl.ds(kk * tok, tok)
            part[n, at] += jnp.dot(spread, jnp.concatenate([top, low], axis=0), preferred_element_type=jnp.float32)

    for s in range(2):
        here = mirrored(s, c)

        @pl.when(here < n - 1)
        def _():
            chain_a(s, c).wait_recv()

        @pl.when(here < n - 2)
        def _():
            chain_b(s, c).wait_recv()
            place(s, True)

        @pl.when(here == n - 2)
        def _():
            place(s, False)

    def last(kk):
        return rdma(fin.at[kk], out_ref.at[:, pl.ds(k * half_d, half_d)], f_ssem.at[kk], f_rsem.at[k],
                    (stage - 1, c * 2 + kk))

    @pl.when(stage > 0)
    def _():
        for kk in range(2):
            fin[kk] = part[n, pl.ds(kk * tok, tok)].astype(jnp.bfloat16)
            last(kk).start()

    @pl.when(stage == stages - 1)
    def _():
        out_ref[...] = jnp.zeros_like(out_ref)

    @pl.when(stage < stages - 1)
    def _():
        for kk in range(2):
            rdma(fin.at[kk], out_ref.at[:, pl.ds(kk * half_d, half_d)], f_ssem.at[kk], f_rsem.at[kk],
                 (stage, me)).wait_recv()

    @pl.when(stage > 0)
    def _():
        for kk in range(2):
            last(kk).wait_send()

    for j in range(1, 2 * n):
        rr_got(j).wait_recv()
        rr_copy(j).wait_send()
        wt_copy(j).wait_send()
    pt_copy.wait_send()
    wp_copy.wait_send()
    for h in range(2):
        nat_copy(h).wait_send()
    for s in range(2):
        here = mirrored(s, c)
        for h in range(2):

            @pl.when(here < n - 1)
            def _():
                own_a(s, h).wait_send()

            @pl.when(here < n - 2)
            def _():
                own_b(s, h).wait_send()

        for d in range(1, n):
            t = real(s, here - d)

            @pl.when(here >= d)
            def _():
                chain_a(s, t).wait_send()
                for h in range(2):
                    pair_a(t, h).wait_send()

                    @pl.when(here < n - 1)
                    def _():
                        fwd_a(s, t, h).wait_send()
                        pair_b(t, h).wait_send()

                    @pl.when(here < n - 2)
                    def _():
                        fwd_b(s, t, h).wait_send()

                @pl.when(here < n - 1)
                def _():
                    chain_b(s, t).wait_send()


def line_local(activations, out_grad, expert_ids, gate_values, w_gate, w_up, w_down):
    x, g, ids, gates = activations[0], out_grad[0], expert_ids[0], gate_values[0]
    n = lax.axis_size("expert") // 2
    tok, feat = x.shape
    hid = w_down.shape[1]
    cap = tok * 3 // 4
    rest = tok - cap
    half_d = feat // 2
    c = lax.axis_index("expert") // 2
    owners = jnp.arange(n, dtype=jnp.int32)
    routed = ids[:, :, None] == owners
    weights = jnp.sum(jnp.where(routed, gates[:, :, None], 0.0), axis=1)
    named = jnp.any(routed, axis=1)
    order = jnp.arange(tok, dtype=jnp.int32)
    before = order[None, :] < order[:, None]

    def places(first):
        ahead = jnp.sum((before & first[None, :]).astype(jnp.int32), axis=1)
        behind = jnp.sum((before & ~first[None, :]).astype(jnp.int32), axis=1)
        return jnp.where(first, ahead, jnp.sum(first.astype(jnp.int32)) + behind)

    spots = jnp.stack([places(named[:, n - 1]), places(named[:, 0]), order])
    moves = spots[:, None, :] == order[None, :, None]
    moves16 = moves.astype(jnp.bfloat16)
    flat = moves16.reshape(3 * tok, tok)
    send_x = jnp.dot(flat, x, preferred_element_type=jnp.float32).astype(x.dtype).reshape(3, tok, feat)
    send_g = jnp.dot(flat, g, preferred_element_type=jnp.float32).astype(g.dtype).reshape(3, tok, feat)
    wt = jnp.sum(jnp.where(moves[:, None], weights.T[None, :, None, :], 0.0), axis=3).reshape(3 * n, tok)
    wt = jnp.pad(wt, ((0, -(3 * n) % 8), (0, 0)))
    pt = jnp.swapaxes(moves16[:2], 1, 2)
    bf, f32 = jnp.bfloat16, jnp.float32
    vmem, dma = pltpu.VMEM, pltpu.SemaphoreType.DMA
    big = max(2 * tok, 2 * n * rest)
    scratch = [
        vmem((n, 2 * cap, feat), bf), vmem((n, 2 * cap, feat), bf),
        vmem((n, 2 * rest, feat), bf), vmem((n, 2 * rest, feat), bf),
        vmem((2 * tok, feat), bf), vmem((2 * tok, feat), bf),
        vmem((feat, 2 * hid), bf), vmem((hid, feat), bf), vmem((half_d, 2 * hid), bf),
        vmem((big, 3 * hid), f32),
        vmem((n + 2, big, 2 * hid), bf), vmem((n + 2, big, 2 * hid), bf),
        vmem((n + 2, big, half_d), f32),
        vmem((2, n, 2 * cap, half_d), bf), vmem((2, n, 2 * rest, half_d), bf),
        vmem((n, 2 * cap, half_d), bf), vmem((n, 2 * rest, half_d), bf),
        vmem((2, tok, half_d), bf),
        vmem((2 * n,) + wt.shape, f32), vmem((2, tok, tok), bf),
        vmem((2 * n, tok, 128), f32), vmem((2 * n, 8, tok), f32),
        dma((3,)), dma((4,)), dma((2,)), dma((2, n, 2)), dma((n, 2)), dma((2 * n, 2)),
        dma((2, n, 2)), dma((n, 2)), dma((2 * n, 2)), dma((2 * n,)), dma((2 * n,)),
        dma, dma, dma, dma, dma((n + 2,)), dma((n + 2,)), dma((n,)), dma((2, n)), dma((n,)), dma((2, n)),
        dma((2 * n,)), dma((2 * n,)), dma((2,)), dma((2,)),
    ]
    in_vmem = pl.BlockSpec(memory_space=pltpu.VMEM)
    passed, rr = pl.pallas_call(
        functools.partial(line_kernel, n, cap),
        out_shape=(jax.ShapeDtypeStruct((tok, feat), bf), jax.ShapeDtypeStruct((2 * n, 8, tok), f32)),
        in_specs=[in_vmem] * 4 + [pl.BlockSpec(memory_space=pl.ANY)] * 3,
        out_specs=(in_vmem, in_vmem),
        scratch_shapes=scratch,
        compiler_params=pltpu.CompilerParams(
            collective_id=0, has_side_effects=True, vmem_limit_bytes=60 * 1024 * 1024
        ),
        name="line",
    )(send_x, send_g, wt, pt, w_gate[0], w_up[0], w_down[0])
    router = jnp.sum(rr[:, 0].reshape(n, 2, tok), axis=1)
    spot = jnp.where(ids > c, spots[0][:, None], jnp.where(ids < c, spots[1][:, None], order[:, None]))
    hit = routed[:, :, :, None] & (spot[:, :, None, None] == order)
    entry = jnp.sum(jnp.where(hit, router, 0.0), axis=(2, 3))
    return (passed[None], entry[None])


def local(*args):
    n = lax.axis_size("expert") // 2
    tok, feat = args[0].shape[1:]
    hid = args[6].shape[1]
    scratch = 2 * n * tok * (feat * 7 + hid * 8) + 6 * feat * hid * 2
    fits = scratch < 40 * 2**20 and tok == 128 and feat % 256 == 0 and hid % 128 == 0
    if fits and n >= 4 and args[2].shape[2] * 2 == n:
        return line_local(*args)
    return routed_local(*args)


def solution(mesh):
    return jax.shard_map(
        local,
        mesh=mesh,
        in_specs=(
            P("pipe", "expert", None),
            P("pipe", "expert", None),
            P("pipe", "expert", None),
            P("pipe", "expert", None),
            P("pipe", None, "expert"),
            P("pipe", None, "expert"),
            P("pipe", "expert", None),
        ),
        out_specs=(P("pipe", "expert", None), P("pipe", "expert", None)),
        check_vma=False,
    )
```

```python
import functools

import jax
import jax.numpy as jnp
from jax import lax
from jax.experimental import pallas as pl
from jax.experimental.pallas import tpu as pltpu
from jax.sharding import PartitionSpec as P


def shifted(block, axis, distance):
    devices = range(lax.axis_size(axis))
    route = [(i - distance, i) for i in devices if i - distance in devices]
    return lax.ppermute(block, axis, route)


def expert_terms(rows_in, rows_grad, gate_cols, up_cols, down_rows):
    contract = (((1,), (1,)), ((), ()))
    gate_pre = jnp.dot(rows_in, gate_cols, preferred_element_type=jnp.float32)
    up_pre = jnp.dot(rows_in, up_cols, preferred_element_type=jnp.float32)
    squash = jax.nn.sigmoid(gate_pre)
    activated = gate_pre * squash
    hidden = (activated * up_pre).astype(jnp.bfloat16)
    back_hidden = lax.dot_general(
        rows_grad, down_rows, contract, preferred_element_type=jnp.float32
    )
    router_part = jnp.sum(hidden.astype(jnp.float32) * back_hidden, axis=1)
    slope = squash * (1.0 + gate_pre * (1.0 - squash))
    grad_gate = (back_hidden * up_pre * slope).astype(jnp.bfloat16)
    grad_up = (back_hidden * activated).astype(jnp.bfloat16)
    route_part = lax.dot_general(grad_gate, gate_cols, contract, preferred_element_type=jnp.float32)
    route_part = route_part + lax.dot_general(
        grad_up, up_cols, contract, preferred_element_type=jnp.float32
    )
    return (route_part, router_part)


def routed_local(activations, out_grad, expert_ids, gate_values, w_gate, w_up, w_down):
    inputs = activations[0]
    grads_out = out_grad[0]
    routes = expert_ids[0]
    weights_gate = gate_values[0]
    gate_local = w_gate[0]
    up_local = w_up[0]
    down_local = w_down[0]
    devices_e = lax.axis_size("expert")
    owners = devices_e // 2
    tokens_dev, top_k = routes.shape
    feat_width = inputs.shape[1]
    capacity = min(tokens_dev * 3 // 4, tokens_dev * top_k * 3 // (2 * owners))
    count_entries = tokens_dev * top_k
    flat_ids = routes.reshape(-1)
    one_hot = (flat_ids[:, None] == jnp.arange(owners, dtype=jnp.int32)[None, :]).astype(jnp.int32)
    slot_rank = jnp.sum((jnp.cumsum(one_hot, axis=0) - 1) * one_hot, axis=1)
    slot_index = flat_ids * capacity + slot_rank
    slot_table = (
        jnp.full((owners * capacity,), count_entries, jnp.int32)
        .at[slot_index]
        .set(jnp.arange(count_entries, dtype=jnp.int32))
    )
    token_of = slot_table // top_k
    pad_row = jnp.zeros((1, feat_width), inputs.dtype)
    send_in = jnp.concatenate([inputs, pad_row], 0)[token_of].reshape(owners, capacity, feat_width)
    send_grad = jnp.concatenate([grads_out, pad_row], 0)[token_of].reshape(
        owners, capacity, feat_width
    )
    full_in = lax.all_to_all(
        jnp.repeat(send_in, 2, axis=0), "expert", split_axis=0, concat_axis=0, tiled=True
    )
    item_count = full_in.shape[1]
    route_part, router_part = expert_terms(
        full_in.reshape(-1, feat_width),
        lax.all_to_all(
            jnp.repeat(send_grad, 2, axis=0), "expert", split_axis=0, concat_axis=0, tiled=True
        ).reshape(-1, feat_width),
        gate_local,
        up_local,
        down_local,
    )
    route_part = route_part.reshape(devices_e, item_count, feat_width)
    router_part = router_part.reshape(devices_e, item_count)
    back_route = lax.all_to_all(
        route_part.astype(jnp.bfloat16), "expert", split_axis=0, concat_axis=0, tiled=True
    ).astype(route_part.dtype)
    back_router = lax.all_to_all(
        router_part.astype(jnp.bfloat16), "expert", split_axis=0, concat_axis=0, tiled=True
    ).astype(router_part.dtype)
    summed = jnp.sum(back_route.reshape(owners, 2, item_count, feat_width), axis=1)
    router_sum = jnp.sum(back_router.reshape(owners, 2, item_count), axis=1)
    route_sum, router_sum = (summed, router_sum)
    entry_route = route_sum.reshape(-1, feat_width)[slot_index]
    entry_router = router_sum.reshape(-1)[slot_index]
    input_grad = jnp.sum(
        weights_gate.reshape(tokens_dev, top_k, 1)
        * entry_route.reshape(tokens_dev, top_k, feat_width),
        axis=1,
    ).astype(jnp.bfloat16)
    passed = shifted(input_grad, "pipe", -1)
    return (passed[None], entry_router.reshape(tokens_dev, top_k)[None])


MESH = pl.DeviceIdType.MESH
NT = (((1,), (1,)), ((), ()))


def line_kernel(
    n, cap, x_ref, g_ref, wt_ref, spot_ref, wg_hbm, wu_hbm, wd_hbm, out_ref, rr_ref,
    sx, sg, pt, xa, ga, xb, gb, xo, go, wgu, wd, wp, pre, gs, gr, part, ca, cb, ta, tb, fin, wts, pts, rl, rs,
    w_sem, o_ssem, rn_sem, a_ssem, a_psem, ra_sem, b_ssem, b_psem, rb_sem, wt_ssem, wt_rsem,
    pt_ssem, pt_rsem, wp_ssem, wp_rsem, g_ssem, g_rsem, ca_ssem, ca_rsem, cb_ssem, cb_rsem,
    rr_ssem, rr_rsem, f_ssem, f_rsem,
):
    stage = lax.axis_index("pipe")
    me = lax.axis_index("expert")
    stages = lax.axis_size("pipe")
    c, k = lax.div(me, 2), lax.rem(me, 2)
    other = 1 - k
    tok = x_ref.shape[0]
    rest = tok - cap
    hid = wd.shape[0]
    half_d = wp.shape[0]
    partner = (stage, c * 2 + other)
    rows_in, send, land_a, land_b, land_o = (x_ref, g_ref), (sx, sg), (xa, ga), (xb, gb), (xo, go)

    def rdma(src, dst, ssem, rsem, dev):
        return pltpu.make_async_remote_copy(
            src_ref=src, dst_ref=dst, send_sem=ssem, recv_sem=rsem, device_id=dev, device_id_type=MESH
        )

    loads = [
        pltpu.make_async_copy(wg_hbm, wgu.at[:, pl.ds(0, hid)], w_sem.at[0]),
        pltpu.make_async_copy(wu_hbm, wgu.at[:, pl.ds(hid, hid)], w_sem.at[1]),
        pltpu.make_async_copy(wd_hbm, wd, w_sem.at[2]),
    ]
    for load in loads:
        load.start()
    rl[...] = jnp.zeros_like(rl)
    order = lax.broadcasted_iota(jnp.int32, (tok, tok), 0)
    for s in range(2):
        move = jnp.where(jnp.broadcast_to(spot_ref[pl.ds(s, 1), :], (tok, tok)) == order, 1.0, 0.0)
        pt[s] = jnp.transpose(move).astype(jnp.bfloat16)
        for h in range(2):
            send[h][s] = jnp.dot(
                move.astype(jnp.bfloat16), rows_in[h][...], preferred_element_type=jnp.float32
            ).astype(jnp.bfloat16)

    barrier = pltpu.get_barrier_semaphore()
    for j in range(1, 2 * n):
        pl.semaphore_signal(barrier, inc=1, device_id=(stage, lax.rem(me + j, 2 * n)), device_id_type=MESH)
    for kk in range(2):

        @pl.when(stage > 0)
        def _():
            pl.semaphore_signal(barrier, inc=1, device_id=(stage - 1, c * 2 + kk), device_id_type=MESH)

        @pl.when(stage < stages - 1)
        def _():
            pl.semaphore_signal(barrier, inc=1, device_id=(stage + 1, c * 2 + kk), device_id_type=MESH)

    near = (stage > 0).astype(jnp.int32) + (stage < stages - 1).astype(jnp.int32)
    pl.semaphore_wait(barrier, 2 * n - 1 + 2 * near)

    def mirrored(s, chip):
        return chip if s == 0 else n - 1 - chip

    def onward(s):
        return (stage, (c + 1 - 2 * s) * 2 + k)

    def backward(s):
        return (stage, (c - 1 + 2 * s) * 2 + k)

    def own_a(s, h):
        return rdma(send[h].at[s, pl.ds(0, cap)], land_a[h].at[c, pl.ds(k * cap, cap)],
                    a_ssem.at[s, c, h], ra_sem.at[me, h], onward(s))

    def fwd_a(s, t, h):
        view = land_a[h].at[t, pl.ds(k * cap, cap)]
        return rdma(view, view, a_ssem.at[s, t, h], ra_sem.at[t * 2 + k, h], onward(s))

    def pair_a(t, h):
        view = land_a[h].at[t, pl.ds(k * cap, cap)]
        return rdma(view, view, a_psem.at[t, h], ra_sem.at[t * 2 + k, h], partner)

    def got_a(t, kk, h):
        view = land_a[h].at[t, pl.ds(kk * cap, cap)]
        return rdma(view, view, a_psem.at[t, h], ra_sem.at[t * 2 + kk, h], partner)

    def own_b(s, h):
        return rdma(send[h].at[s, pl.ds(cap, rest)], land_b[h].at[c, pl.ds(k * rest, rest)],
                    b_ssem.at[s, c, h], rb_sem.at[me, h], onward(s))

    def fwd_b(s, t, h):
        view = land_b[h].at[t, pl.ds(k * rest, rest)]
        return rdma(view, view, b_ssem.at[s, t, h], rb_sem.at[t * 2 + k, h], onward(s))

    def pair_b(t, h):
        view = land_b[h].at[t, pl.ds(k * rest, rest)]
        return rdma(view, view, b_psem.at[t, h], rb_sem.at[t * 2 + k, h], partner)

    def got_b(t, kk, h):
        view = land_b[h].at[t, pl.ds(kk * rest, rest)]
        return rdma(view, view, b_psem.at[t, h], rb_sem.at[t * 2 + kk, h], partner)

    def nat_copy(h):
        return rdma(rows_in[h], land_o[h].at[pl.ds(k * tok, tok)], o_ssem.at[h], rn_sem.at[h], partner)

    def nat_here(h):
        return pltpu.make_async_copy(rows_in[h], land_o[h].at[pl.ds(k * tok, tok)], o_ssem.at[2 + h])

    def wt_copy(j):
        return rdma(wt_ref, wts.at[me], wt_ssem.at[j], wt_rsem.at[me], (stage, lax.rem(me + j, 2 * n)))

    def wt_got(j):
        src = lax.rem(me + j, 2 * n)
        return rdma(wt_ref, wts.at[src], wt_ssem.at[j], wt_rsem.at[src], (stage, src))

    pt_copy = rdma(pt, pts, pt_ssem, pt_rsem, partner)
    wp_copy = rdma(wgu.at[pl.ds(other * half_d, half_d)], wp, wp_ssem, wp_rsem, partner)

    for s in range(2):

        @pl.when(mirrored(s, c) < n - 1)
        def _():
            for h in range(2):
                own_a(s, h).start()

    for h in range(2):
        nat_copy(h).start()
        nat_here(h).start()
    for j in range(1, 2 * n):
        wt_copy(j).start()
    wts[me] = wt_ref[...]
    pt_copy.start()
    for load in loads:
        load.wait()
    wp_copy.start()

    def swap(slot, rows):
        return rdma(gs.at[slot, pl.ds(0, rows)], gr.at[slot, pl.ds(0, rows)], g_ssem.at[slot], g_rsem.at[slot], partner)

    def column(v):
        return jnp.transpose(jnp.broadcast_to(v, (v.shape[1], v.shape[1])))[:, :1]

    def terms(x_view, g_view, rows, slot, put_router):
        step = 256 if (2 * hid) % 256 == 0 else 128

        @pl.loop(0, 2 * hid // step)
        def _(j):
            cols = pl.ds(pl.multiple_of(j * step, step), step)
            pre[pl.ds(0, rows), cols] = jnp.dot(x_view[...], wgu[:, cols], preferred_element_type=jnp.float32)

        pre[pl.ds(0, rows), pl.ds(2 * hid, hid)] = lax.dot_general(
            g_view[...], wd[...], NT, preferred_element_type=jnp.float32
        )
        chunk = 32

        @pl.loop(0, rows // chunk)
        def _(i):
            at = pl.ds(pl.multiple_of(i * chunk, chunk), chunk)
            gate_pre = pre[at, pl.ds(0, hid)]
            up_pre = pre[at, pl.ds(hid, hid)]
            back = pre[at, pl.ds(2 * hid, hid)]
            squash = jax.nn.sigmoid(gate_pre)
            activated = gate_pre * squash
            hidden = (activated * up_pre).astype(jnp.bfloat16)
            router = jnp.sum(hidden.astype(jnp.float32) * back, axis=1, keepdims=True)
            slope = squash * (1.0 + gate_pre * (1.0 - squash))
            gs[slot, at, pl.ds(0, hid)] = (back * up_pre * slope).astype(jnp.bfloat16)
            gs[slot, at, pl.ds(hid, hid)] = (back * activated).astype(jnp.bfloat16)
            pre[at, pl.ds(0, 128)] = jnp.broadcast_to(router, (chunk, 128))

        swap(slot, rows).start()
        put_router()

    def products(rows, slot, weight):
        step = 256 if half_d % 256 == 0 else 128

        @pl.loop(0, half_d // step)
        def _(j):
            cols = pl.ds(pl.multiple_of(j * step, step), step)
            mine = pl.ds(pl.multiple_of(k * half_d + j * step, step), step)
            part[slot, pl.ds(0, rows), cols] = lax.dot_general(
                gs[slot, pl.ds(0, rows)], wgu[mine, :], NT, preferred_element_type=jnp.float32
            )

        swap(slot, rows).wait()

        @pl.loop(0, half_d // step)
        def _(j):
            cols = pl.ds(pl.multiple_of(j * step, step), step)
            total = part[slot, pl.ds(0, rows), cols] + lax.dot_general(
                gr[slot, pl.ds(0, rows)], wp[cols, :], NT, preferred_element_type=jnp.float32
            )
            part[slot, pl.ds(0, rows), cols] = total * weight

    def row_weights(t, base, lo, size):
        cols = [column(wts[t * 2 + kk, pl.ds(base + c, 1), :])[lo:lo + size] for kk in range(2)]
        return jnp.concatenate(cols, axis=0)

    for h in range(2):
        rdma(rows_in[h], land_o[h].at[pl.ds(other * tok, tok)], o_ssem.at[h], rn_sem.at[h], partner).wait_recv()
        nat_here(h).wait()
    for j in range(1, 2 * n):
        wt_got(j).wait_recv()

    def own_router():
        for kk in range(2):
            rl[c * 2 + kk] = pre[pl.ds(kk * tok, tok), pl.ds(0, 128)]

    terms(xo, go, 2 * tok, n, own_router)
    wp_copy.wait_recv()
    products(2 * tok, n, row_weights(c, 2 * n, 0, tok))

    quarter = cap // 2

    def chain_a(s, t, q):
        at = pl.ds(q * quarter, quarter)
        return rdma(ta.at[t, at], ca.at[s, t, at], ca_ssem.at[t, q], ca_rsem.at[s, t, q], backward(s))

    def chain_b(s, t):
        return rdma(tb.at[t], cb.at[s, t], cb_ssem.at[t], cb_rsem.at[s, t], backward(s))

    def real(s, chip):
        return chip if s == 0 else n - 1 - chip

    def chain_step(at):
        for s in range(2):
            here = mirrored(s, c)
            target = 2 * (n - 1) - here - at
            t = real(s, target)

            @pl.when((target >= 0) & (target < here))
            def _():
                for q in range(4):
                    at_q = pl.ds(q * quarter, quarter)

                    @pl.when(here < n - 1)
                    def _():
                        chain_a(s, t, q).wait_recv()
                        ta[t, at_q] = (part[t, at_q] + ca[s, t, at_q].astype(jnp.float32)).astype(jnp.bfloat16)

                    @pl.when(here == n - 1)
                    def _():
                        ta[t, at_q] = part[t, at_q].astype(jnp.bfloat16)

                    chain_a(s, t, q).start()

    @pl.loop(1, n)
    def _(d):
        for s in range(2):
            here = mirrored(s, c)
            t = real(s, here - d)

            @pl.when(here >= d)
            def _():
                for h in range(2):
                    got_a(t, k, h).wait_recv()

                    @pl.when(here < n - 1)
                    def _():
                        fwd_a(s, t, h).start()

                    pair_a(t, h).start()

        for s in range(2):
            here = mirrored(s, c)

            @pl.when((here < n - 2) & (d == jnp.maximum(here, 1)))
            def _():
                for h in range(2):
                    own_b(s, h).start()

        @pl.loop(0, 2)
        def _(side):
            t = jnp.where(side == 0, c - d, c + d)

            @pl.when((t >= 0) & (t < n))
            def _():
                for h in range(2):
                    got_a(t, other, h).wait_recv()

                def put_router():
                    for kk in range(2):
                        rl[t * 2 + kk, pl.ds(0, cap)] = pre[pl.ds(kk * cap, cap), pl.ds(0, 128)]

                terms(xa.at[t], ga.at[t], 2 * cap, t, put_router)
                products(2 * cap, t, row_weights(t, side * n, 0, cap))

        for s in range(2):
            here = mirrored(s, c)
            back = jnp.where(here < n - 2, d, d - 1)
            t = real(s, here - back)

            @pl.when((here >= back) & (back > 0) & (here < n - 1))
            def _():
                for h in range(2):
                    got_b(t, k, h).wait_recv()

                    @pl.when(here < n - 2)
                    def _():
                        fwd_b(s, t, h).start()

                    pair_b(t, h).start()

        chain_step(d)

    inner = (c > 0) & (c < n - 1)

    @pl.when(inner)
    def _():
        for j in range(1, n):
            t = lax.rem(c + j, n)
            for h in range(2):
                got_b(t, other, h).wait_recv()

        def put_router():
            @pl.loop(0, n)
            def _(t):
                @pl.when(t != c)
                def _():
                    for kk in range(2):
                        rl[t * 2 + kk, pl.ds(cap, rest)] = pre[
                            pl.ds(pl.multiple_of(t * 2 * rest + kk * rest, rest), rest), pl.ds(0, 128)]

        rows_b = n * 2 * rest
        terms(xb.reshape(rows_b, xb.shape[2]), gb.reshape(rows_b, gb.shape[2]), rows_b, n + 1, put_router)
        weights = [row_weights(t, jnp.where(t < c, 0, n), cap, rest) for t in range(n)]
        products(rows_b, n + 1, jnp.concatenate(weights, axis=0))

    def chain_step_b(here_at):
        for s in range(2):
            here = mirrored(s, c)

            @pl.when(here == here_at)
            def _():
                for target in range(here_at):
                    t = real(s, target)
                    mine = part[n + 1, pl.ds(t * 2 * rest, 2 * rest)]
                    if here_at < n - 2:
                        chain_b(s, t).wait_recv()
                        mine = mine + cb[s, t].astype(jnp.float32)
                    tb[t] = mine.astype(jnp.bfloat16)
                    chain_b(s, t).start()

    for here_at in range(n - 2, 0, -1):
        chain_step_b(here_at)
    for at in range(n, 2 * (n - 1)):
        chain_step(at)

    def rr_copy(j):
        dst = lax.rem(me + j, 2 * n)
        return rdma(rs.at[dst], rr_ref.at[me], rr_ssem.at[j], rr_rsem.at[me], (stage, dst))

    def rr_got(j):
        src = lax.rem(me + j, 2 * n)
        return rdma(rs.at[src], rr_ref.at[src], rr_ssem.at[j], rr_rsem.at[src], (stage, src))

    @pl.loop(0, 2 * n)
    def _(src):
        rs[src] = jnp.transpose(rl[src])[:8]

    for j in range(1, 2 * n):
        rr_copy(j).start()
    rr_ref[me] = rs[me]

    pt_copy.wait_recv()

    def place(s, kk, rows_b):
        top = ca[s, c, pl.ds(kk * cap, cap)]
        low = cb[s, c, pl.ds(kk * rest, rest)] if rows_b else jnp.zeros((rest, half_d), jnp.bfloat16)
        spread = jnp.where(kk == k, pt[s], pts[s])
        part[n, pl.ds(kk * tok, tok)] += jnp.dot(
            spread, jnp.concatenate([top, low], axis=0), preferred_element_type=jnp.float32
        )

    def last(kk):
        return rdma(fin.at[kk], out_ref.at[:, pl.ds(k * half_d, half_d)], f_ssem.at[kk], f_rsem.at[k],
                    (stage - 1, c * 2 + kk))

    for s in range(2):

        @pl.when(mirrored(s, c) < n - 2)
        def _():
            chain_b(s, c).wait_recv()

    for kk in range(2):
        for s in range(2):
            here = mirrored(s, c)

            @pl.when(here < n - 1)
            def _():
                for q in range(2):
                    chain_a(s, c, 2 * kk + q).wait_recv()

            @pl.when(here < n - 2)
            def _():
                place(s, kk, True)

            @pl.when(here == n - 2)
            def _():
                place(s, kk, False)

        @pl.when(stage > 0)
        def _():
            fin[kk] = part[n, pl.ds(kk * tok, tok)].astype(jnp.bfloat16)
            last(kk).start()

    @pl.when(stage == stages - 1)
    def _():
        out_ref[...] = jnp.zeros_like(out_ref)

    @pl.when(stage < stages - 1)
    def _():
        for kk in range(2):
            rdma(fin.at[kk], out_ref.at[:, pl.ds(kk * half_d, half_d)], f_ssem.at[kk], f_rsem.at[kk],
                 (stage, me)).wait_recv()

    @pl.when(stage > 0)
    def _():
        for kk in range(2):
            last(kk).wait_send()

    for j in range(1, 2 * n):
        rr_got(j).wait_recv()
        rr_copy(j).wait_send()
        wt_copy(j).wait_send()
    pt_copy.wait_send()
    wp_copy.wait_send()
    for h in range(2):
        nat_copy(h).wait_send()
    for s in range(2):
        here = mirrored(s, c)
        for h in range(2):

            @pl.when(here < n - 1)
            def _():
                own_a(s, h).wait_send()

            @pl.when(here < n - 2)
            def _():
                own_b(s, h).wait_send()

        for d in range(1, n):
            t = real(s, here - d)

            @pl.when(here >= d)
            def _():
                for q in range(4):
                    chain_a(s, t, q).wait_send()
                for h in range(2):
                    pair_a(t, h).wait_send()

                    @pl.when(here < n - 1)
                    def _():
                        fwd_a(s, t, h).wait_send()
                        pair_b(t, h).wait_send()

                    @pl.when(here < n - 2)
                    def _():
                        fwd_b(s, t, h).wait_send()

                @pl.when(here < n - 1)
                def _():
                    chain_b(s, t).wait_send()


def line_local(activations, out_grad, expert_ids, gate_values, w_gate, w_up, w_down):
    x, g, ids, gates = activations[0], out_grad[0], expert_ids[0], gate_values[0]
    n = lax.axis_size("expert") // 2
    tok, feat = x.shape
    hid = w_down.shape[1]
    cap = tok * 3 // 4
    rest = tok - cap
    half_d = feat // 2
    c = lax.axis_index("expert") // 2
    owners = jnp.arange(n, dtype=jnp.int32)
    routed = ids[:, :, None] == owners
    weights = jnp.sum(jnp.where(routed, gates[:, :, None], 0.0), axis=1)
    named = jnp.any(routed, axis=1)
    order = jnp.arange(tok, dtype=jnp.int32)
    before = order[None, :] < order[:, None]

    def places(first):
        ahead = jnp.sum((before & first[None, :]).astype(jnp.int32), axis=1)
        behind = jnp.sum((before & ~first[None, :]).astype(jnp.int32), axis=1)
        return jnp.where(first, ahead, jnp.sum(first.astype(jnp.int32)) + behind)

    spots = jnp.stack([places(named[:, n - 1]), places(named[:, 0]), order])
    moves = spots[:, None, :] == order[None, :, None]
    wt = jnp.sum(jnp.where(moves[:, None], weights.T[None, :, None, :], 0.0), axis=3).reshape(3 * n, tok)
    wt = jnp.pad(wt, ((0, -(3 * n) % 8), (0, 0)))
    bf, f32 = jnp.bfloat16, jnp.float32
    vmem, dma = pltpu.VMEM, pltpu.SemaphoreType.DMA
    big = max(2 * tok, 2 * n * rest)
    scratch = [
        vmem((2, tok, feat), bf), vmem((2, tok, feat), bf), vmem((2, tok, tok), bf),
        vmem((n, 2 * cap, feat), bf), vmem((n, 2 * cap, feat), bf),
        vmem((n, 2 * rest, feat), bf), vmem((n, 2 * rest, feat), bf),
        vmem((2 * tok, feat), bf), vmem((2 * tok, feat), bf),
        vmem((feat, 2 * hid), bf), vmem((hid, feat), bf), vmem((half_d, 2 * hid), bf),
        vmem((big, 3 * hid), f32),
        vmem((n + 2, big, 2 * hid), bf), vmem((n + 2, big, 2 * hid), bf),
        vmem((n + 2, big, half_d), f32),
        vmem((2, n, 2 * cap, half_d), bf), vmem((2, n, 2 * rest, half_d), bf),
        vmem((n, 2 * cap, half_d), bf), vmem((n, 2 * rest, half_d), bf),
        vmem((2, tok, half_d), bf),
        vmem((2 * n,) + wt.shape, f32), vmem((2, tok, tok), bf),
        vmem((2 * n, tok, 128), f32), vmem((2 * n, 8, tok), f32),
        dma((3,)), dma((4,)), dma((2,)), dma((2, n, 2)), dma((n, 2)), dma((2 * n, 2)),
        dma((2, n, 2)), dma((n, 2)), dma((2 * n, 2)), dma((2 * n,)), dma((2 * n,)),
        dma, dma, dma, dma, dma((n + 2,)), dma((n + 2,)), dma((n, 4)), dma((2, n, 4)), dma((n,)), dma((2, n)),
        dma((2 * n,)), dma((2 * n,)), dma((2,)), dma((2,)),
    ]
    in_vmem = pl.BlockSpec(memory_space=pltpu.VMEM)
    passed, rr = pl.pallas_call(
        functools.partial(line_kernel, n, cap),
        out_shape=(jax.ShapeDtypeStruct((tok, feat), bf), jax.ShapeDtypeStruct((2 * n, 8, tok), f32)),
        in_specs=[in_vmem] * 4 + [pl.BlockSpec(memory_space=pl.ANY)] * 3,
        out_specs=(in_vmem, in_vmem),
        scratch_shapes=scratch,
        compiler_params=pltpu.CompilerParams(
            collective_id=0, has_side_effects=True, vmem_limit_bytes=60 * 1024 * 1024
        ),
        name="line",
    )(x, g, wt, spots, w_gate[0], w_up[0], w_down[0])
    router = jnp.sum(rr[:, 0].reshape(n, 2, tok), axis=1)
    spot = jnp.where(ids > c, spots[0][:, None], jnp.where(ids < c, spots[1][:, None], order[:, None]))
    hit = routed[:, :, :, None] & (spot[:, :, None, None] == order)
    entry = jnp.sum(jnp.where(hit, router, 0.0), axis=(2, 3))
    return (passed[None], entry[None])


def local(*args):
    n = lax.axis_size("expert") // 2
    tok, feat = args[0].shape[1:]
    hid = args[6].shape[1]
    scratch = 2 * n * tok * (feat * 7 + hid * 8) + 6 * feat * hid * 2
    fits = scratch < 40 * 2**20 and tok == 128 and feat % 256 == 0 and hid % 128 == 0
    if fits and n >= 4 and args[2].shape[2] * 2 == n:
        return line_local(*args)
    return routed_local(*args)


def solution(mesh):
    return jax.shard_map(
        local,
        mesh=mesh,
        in_specs=(
            P("pipe", "expert", None),
            P("pipe", "expert", None),
            P("pipe", "expert", None),
            P("pipe", "expert", None),
            P("pipe", None, "expert"),
            P("pipe", None, "expert"),
            P("pipe", "expert", None),
        ),
        out_specs=(P("pipe", "expert", None), P("pipe", "expert", None)),
        check_vma=False,
    )
```
